32 devices in a mesh: row: 8 (over y, x, core), col: 4 (over z).
Axes of the slice: x: 2, y: 2, z: 4, core: 2. Of those that a mesh axis runs over, the one named last changes fastest.
Arguments:
- amplitudes: float32 [512, 32, 32, 32], P('col', 'row'), may hold values from -6 to 6
- integrals: float32 [1024, 16384], P('col', 'row'), may hold values from -0.1875 to 0.1875
- occ_energy: float32 [32], replicated, may hold values from -2 to -0.5
- vir_energy: float32 [512], replicated, may hold values from 0.3 to 3
Outputs:
- residual: float32 [16384, 16384], P('col', 'row')
The draws below stay inside these ranges and needn't reach their ends.
All inputs are finite; a program needn't handle non-finite values.
Results may differ from the reference program's by a relative error of at most 0.00007.
Values sent between devices are 32-bit elements; how exact they have to be, the bound alone decides.
A program may use at most 192 MiB of HBM per device.

```python
import jax
import jax.numpy as jnp
from jax import lax

V = 512
O = 32
KWIN = 1024
NOV = 16384
CWIN = 32


def block_scale(own_key, shape, cuts, least, high):
    factor_of = 1.0
    for dim, parts in cuts:
        steps = jax.random.uniform(jax.random.fold_in(jax.random.fold_in(own_key, 6), dim), (parts,), jnp.float32, least / len(cuts), high / len(cuts))
        factor_of = factor_of * jnp.repeat(jnp.exp(steps), shape[dim] // parts).reshape((-1,) + (1,) * (len(shape) - 1 - dim))
    return factor_of


def gaussian(key, dims, spread, most, cuts=(), dtype=jnp.bfloat16):
    result = spread * jax.random.normal(key, dims, jnp.float32)
    if cuts:
        result = result * block_scale(key, dims, cuts, -0.22, 0.18)
    return jnp.clip(result, -most, most).astype(dtype)


def setup_inputs(seed: int = 0) -> dict:
    arg_keys = jax.random.split(jax.random.key(seed), 5)
    amplitudes = gaussian(arg_keys[0], (V, O, CWIN, O), 1.0, 6.0, ((0, 4), (1, 8)), jnp.float32)
    integrals = gaussian(arg_keys[1], (KWIN, NOV), KWIN ** -0.5, 0.1875, ((0, 4), (1, 8)), jnp.float32)
    occ_energy = jnp.clip(jax.random.uniform(arg_keys[2], (O,), jnp.float32, -2.0, -0.5), -2.0, -0.5)
    vir_energy = jnp.clip(jax.random.uniform(arg_keys[3], (V,), jnp.float32, 0.3, 3.0), 0.3, 3.0)
    return {"amplitudes": amplitudes, "integrals": integrals, "occ_energy": occ_energy, "vir_energy": vir_energy}


def reference(amplitudes, integrals, occ_energy, vir_energy):
    amp_matrix = amplitudes.reshape(V * O, KWIN)
    contracted = jnp.dot(amp_matrix, integrals, preferred_element_type=jnp.float32, precision=lax.Precision.HIGHEST)
    gap = (vir_energy[:, None] - occ_energy[None, :]).reshape(V * O)
    return contracted / (gap[:, None] + gap[None, :])
```

```python
import jax
import jax.numpy as jnp
from jax import lax
from jax.experimental import pallas as pl
from jax.experimental.pallas import tpu as pltpu
from jax.sharding import PartitionSpec as P


CUTS = (0, 4, 6, 7, 8)
A_CUTS = 4
W_CUTS = 4
LANES = 128
PAD = 8
GROUP = 8


def masks(size):
    return [1 << j for j in range(size.bit_length() - 1)]


def split(x):
    high = x.astype(jnp.bfloat16)
    return high, (x - high.astype(jnp.float32)).astype(jnp.bfloat16)


def across(index, bit):
    return index + bit - 2 * bit * (index // bit % 2)


def doubling(me, bits):
    held, flows, partners = [me], [], [across(me, bit) for bit in bits]
    for s, bit in enumerate(bits):
        for j, x in enumerate(list(held)):
            flows.append((s, j))
            held.append(across(x, bit))
    return partners, flows, held


def gather_kernel(
    rows_size, parts, amp_ref, w_ref, vir_ref, down_ref, along_ref, high_ref, low_ref, wide_ref, row_ref, col_ref,
    land, mixed, high, low, own_w, row_gap, col_gap, send, recv, swap_send, swap_recv, w_send, w_recv, local
):
    row, col = lax.axis_index("row"), lax.axis_index("col")
    own, depth, virtuals = amp_ref.shape
    occupied = own * rows_size
    cut = high.shape[1]
    cuts = depth // cut
    w_rows = w_ref.shape[0]
    w_width = wide_ref.shape[1] // W_CUTS

    def chip_bits(device):
        chip = masks(rows_size)[1:]
        odd = device % 2
        return [a + odd * (b - a) for a, b in zip(chip, chip[::-1])]

    sibling = across(row, 1)
    partners, flows, held = doubling(row, chip_bits(row))
    sibling_held = doubling(sibling, chip_bits(sibling))[2]
    w_partners, w_flows, w_held = doubling(col, masks(parts)[::-1])

    barrier = pltpu.get_barrier_semaphore()
    for device in partners + [sibling]:
        pl.semaphore_signal(barrier, inc=1, device_id=(device, col), device_id_type=pl.DeviceIdType.MESH)
    for device in w_partners:
        pl.semaphore_signal(barrier, inc=1, device_id=(row, device), device_id_type=pl.DeviceIdType.MESH)
    pl.semaphore_wait(barrier, len(partners) + 1 + len(w_partners))

    def part(ref, j):
        return ref.at[:, pl.ds(pl.multiple_of(j * cut, cut), cut), :]

    def remote(source, target, send_sem, recv_sem, device):
        return pltpu.make_async_remote_copy(
            src_ref=source, dst_ref=target, send_sem=send_sem, recv_sem=recv_sem,
            device_id=device, device_id_type=pl.DeviceIdType.MESH,
        )

    def flow(j, e):
        s, q = flows[e]
        source = amp_ref if q == 0 else land.at[held[q]]
        return remote(part(source, j), part(land.at[held[q]], j), send.at[j, e], recv.at[j, e], (partners[s], col))

    def arrival(j, e):
        block = part(land.at[held[e + 1]], j)
        return remote(block, block, send.at[j, e], recv.at[j, e], (sibling, col))

    def across_chip(j, q):
        source = amp_ref if q == 0 else land.at[held[q]]
        return remote(part(source, j), part(land.at[held[q]], j), swap_send.at[j, q], swap_recv.at[j, q], (sibling, col))

    def chip_arrival(j, q):
        block = part(land.at[sibling_held[q]], j)
        return remote(block, block, swap_send.at[j, q], swap_recv.at[j, q], (sibling, col))

    def w_span(k):
        return pl.ds(pl.multiple_of(k * w_width, w_width), w_width)

    def w_block(k, q):
        return wide_ref.at[pl.ds(pl.multiple_of(w_held[q] * w_rows, w_rows), w_rows), w_span(k)]

    def w_flow(k, e):
        s, q = w_flows[e]
        source = w_ref.at[:, w_span(k)] if q == 0 else w_block(k, q)
        return remote(source, w_block(k, q), w_send.at[k, e], w_recv.at[k, e], (row, w_partners[s]))

    def w_arrival(k, e):
        block = w_block(k, e + 1)
        return remote(block, block, w_send.at[k, e], w_recv.at[k, e], (row, w_partners[0]))

    def issue(j):
        for e, (s, q) in enumerate(flows):
            if q == 0:
                flow(j, e).start()
        across_chip(j, 0).start()

    issue(0)
    for s in range(len(w_partners)):
        for k in range(W_CUTS):
            for e, (t, q) in enumerate(w_flows):
                if q == 0 and t == s:
                    w_flow(k, e).start()
        if s == 0 and cuts > 1:
            issue(1)
    mine = pltpu.make_async_copy(amp_ref, land.at[row], local.at[0])
    mine.start()
    w_in = pltpu.make_async_copy(w_ref.at[:, pl.ds(0, W_CUTS * w_width)], own_w, local.at[1])
    w_in.start()
    mine.wait()
    w_in.wait()
    w_out = pltpu.make_async_copy(
        own_w, wide_ref.at[pl.ds(pl.multiple_of(col * w_rows, w_rows), w_rows), :], local.at[1]
    )
    w_out.start()

    blocks, stride = cut // LANES, occupied + PAD
    w_relayed = sorted({q - 1 for _, q in w_flows if q})

    def place(device, j):
        for i in range(own):
            for block in range(blocks):
                x = land[device, i, pl.ds(pl.multiple_of(j * cut + block * LANES, LANES), LANES), :]
                mixed[block, pl.ds(device * own + i, virtuals, stride=stride), :] = jnp.swapaxes(x, 0, 1)

    def store(j):
        span = pl.ds(pl.multiple_of(j * cut, cut), cut)
        return [
            pltpu.make_async_copy(high, high_ref.at[:, span], local.at[2]),
            pltpu.make_async_copy(low, low_ref.at[:, span], local.at[3]),
        ]

    gap_copies = [
        pltpu.make_async_copy(row_gap, row_ref, local.at[4]),
        pltpu.make_async_copy(col_gap, col_ref, local.at[5]),
    ]

    def gaps():
        @pl.loop(0, virtuals)
        def _(a):
            rows = pl.ds(pl.multiple_of(a * occupied, occupied), occupied)
            row_gap[rows, :] = vir_ref[col * virtuals + a] - down_ref[...]

        columns = col_gap.shape[1]
        per = LANES // occupied
        place_of = lax.broadcasted_iota(jnp.int32, (8, LANES), 1)

        @pl.loop(0, columns // LANES)
        def _(n):
            first = row * (columns // occupied) + n * per
            value = jnp.full((8, LANES), vir_ref[first], jnp.float32)
            for v in range(1, per):
                value = jnp.where(place_of >= v * occupied, vir_ref[first + v], value)
            col_gap[:, pl.ds(pl.multiple_of(n * LANES, LANES), LANES)] = value - along_ref[...]

        for copy in gap_copies:
            copy.start()

    relayed = sorted({q - 1 for _, q in flows if q})

    def forward(j):
        for e in relayed:
            arrival(j, e).wait_recv()
            for f, (t, p) in enumerate(flows):
                if p == e + 1:
                    flow(j, f).start()
            across_chip(j, e + 1).start()

        @pl.when(j + 2 < cuts)
        def _():
            issue(j + 2)

    forward(0)
    gaps()

    @pl.loop(0, cuts)
    def _(j):
        @pl.when(j + 1 < cuts)
        def _():
            forward(j + 1)

        place(row, j)
        for e in relayed:
            place(held[e + 1], j)
        for n in range(2):
            k = 2 * j + n

            @pl.when(k < W_CUTS)
            def _(k=k):
                for e in w_relayed:
                    w_arrival(k, e).wait_recv()
                    for f, (t, p) in enumerate(w_flows):
                        if p == e + 1:
                            w_flow(k, f).start()
        for e in range(len(flows)):
            if e not in relayed:
                arrival(j, e).wait_recv()
                across_chip(j, e + 1).start()
                place(held[e + 1], j)
        for q in range(len(held)):
            chip_arrival(j, q).wait_recv()
            place(sibling_held[q], j)

        @pl.when(j > 0)
        def _():
            for copy in store(j):
                copy.wait()

        for block in range(blocks):
            lanes = pl.ds(block * LANES, LANES)

            @pl.loop(0, virtuals // GROUP)
            def _(g):
                for n in range(GROUP):
                    a = g * GROUP + n
                    rows = pl.ds(pl.multiple_of(a * occupied, occupied), occupied)
                    x = mixed[block, pl.ds(pl.multiple_of(a * stride, 8), occupied), :]
                    high[rows, lanes], low[rows, lanes] = split(x)

        for copy in store(j):
            copy.start()

    for copy in store(cuts - 1):
        copy.wait()
    w_out.wait()
    for copy in gap_copies:
        copy.wait()
    for k in range(W_CUTS):
        for e in range(len(w_flows)):
            if e not in w_relayed:
                w_arrival(k, e).wait_recv()
    for j in range(cuts):
        for e in range(len(flows)):
            flow(j, e).wait_send()
        for q in range(len(held)):
            across_chip(j, q).wait_send()
    for k in range(W_CUTS):
        for e in range(len(w_flows)):
            w_flow(k, e).wait_send()


def gather(amplitudes, integrals, occ_energy, vir_energy, width):
    own, depth, virtuals = amplitudes.shape
    rows_size, parts = lax.axis_size("row"), lax.axis_size("col")
    occupied = own * rows_size
    cut = depth // A_CUTS
    flows, held, w_flows = rows_size // 2 - 1, rows_size // 2, parts - 1
    terms = jax.ShapeDtypeStruct((occupied * virtuals, depth), jnp.bfloat16)
    wide = jax.ShapeDtypeStruct((parts * integrals.shape[0], width), jnp.float32)
    down = jax.ShapeDtypeStruct((occupied * virtuals, LANES), jnp.float32)
    along = jax.ShapeDtypeStruct((8, integrals.shape[1]), jnp.float32)
    sent = 4 * (amplitudes.size * flows + parts * integrals.shape[0] * width)
    dma = pltpu.SemaphoreType.DMA
    return pl.pallas_call(
        lambda *refs: gather_kernel(rows_size, parts, *refs),
        in_specs=[pl.BlockSpec(memory_space=pl.ANY)] * 2
        + [pl.BlockSpec(memory_space=pltpu.SMEM)] + [pl.BlockSpec(memory_space=pltpu.VMEM)] * 2,
        out_specs=[pl.BlockSpec(memory_space=pl.ANY)] * 5,
        out_shape=[terms, terms, wide, down, along],
        scratch_shapes=[
            pltpu.VMEM((rows_size, own, depth, virtuals), jnp.float32),
            pltpu.VMEM((cut // LANES, virtuals * (occupied + PAD), LANES), jnp.float32),
            pltpu.VMEM((occupied * virtuals, cut), jnp.bfloat16),
            pltpu.VMEM((occupied * virtuals, cut), jnp.bfloat16),
            pltpu.VMEM((integrals.shape[0], width), jnp.float32),
            pltpu.VMEM(down.shape, jnp.float32),
            pltpu.VMEM(along.shape, jnp.float32),
            dma((A_CUTS, flows)), dma((A_CUTS, flows)),
            dma((A_CUTS, held)), dma((A_CUTS, held)),
            dma((W_CUTS, w_flows)), dma((W_CUTS, w_flows)),
            dma((6,)),
        ],
        compiler_params=pltpu.CompilerParams(
            collective_id=0, has_side_effects=True, vmem_limit_bytes=60 * 1024 * 1024
        ),
        cost_estimate=pl.CostEstimate(flops=0, bytes_accessed=sent * 8, transcendentals=0),
        name="gather",
    )(
        amplitudes,
        integrals,
        vir_energy,
        jnp.broadcast_to(occ_energy[:, None], (occupied, LANES)),
        jnp.broadcast_to(jnp.tile(occ_energy, LANES // occupied)[None, :], (8, LANES)),
    )


def product_kernel(groups, parts, steps, aliased, where_ref, *refs):
    count, halves = groups * parts, len(steps)
    pieces, refs = refs[:count], refs[count:]
    terms, refs = refs[: 2 * halves], refs[2 * halves :]
    row_ref, col_ref = refs[:2]
    out_ref, w_ref = refs[2 + aliased :]
    depth, width = pieces[0].shape
    whole = parts * depth
    m = pl.program_id(0)

    @pl.when(m == 0)
    def _():
        for j, piece in enumerate(pieces):
            start = pl.multiple_of(where_ref[j % parts] * depth, depth)
            lanes = pl.ds(j // parts * width, width)
            w_high, w_low = split(piece[...])
            w_ref[pl.ds(start, depth), lanes] = w_high
            w_ref[pl.ds(start + whole, depth), lanes] = w_high
            w_ref[pl.ds(start + 2 * whole, depth), lanes] = w_low

    def multiply(high_ref, low_ref):
        high = high_ref[...]
        both = jnp.concatenate([high, low_ref[...], high], axis=1)
        total = jnp.dot(both, w_ref[...], preferred_element_type=jnp.float32)
        out_ref[...] = total / (row_ref[:, :1] + col_ref[:1, :])

    if halves == 1:
        multiply(*terms)
    else:
        stop = 0
        for h, step in enumerate(steps):
            start, stop = stop, stop + step
            pl.when((m >= start) & (m < stop))(lambda h=h: multiply(terms[2 * h], terms[2 * h + 1]))


def product(where, chunks, halves, row_gap, col_gap, out, shape, top, start):
    groups, parts = len(chunks), len(chunks[0])
    depth, width = chunks[0][0].shape
    total = groups * width
    whole = halves[0][0].shape[1]
    tile = min(512 if total > 256 else 1024, halves[0][0].shape[0])
    steps = [high.shape[0] // tile for high, _ in halves]
    rows = sum(steps) * tile
    first, chunk = top // tile, start // total
    aliased = 0 if out is None else 1
    in_specs = [pl.BlockSpec((depth, width), lambda m, s: (0, 0), pipeline_mode=pl.Buffered(1))] * (groups * parts)
    before = 0
    for step in steps:
        index = lambda m, s, before=before, step=step: (jnp.clip(m - before, 0, step - 1), 0)
        in_specs += [pl.BlockSpec((tile, whole), index)] * 2
        before += step
    in_specs += [pl.BlockSpec((tile, LANES), lambda m, s: (m + first, 0))]
    in_specs += [pl.BlockSpec((8, total), lambda m, s: (0, chunk))]
    operands = [where, *(piece for pieces in chunks for piece in pieces)]
    operands += [term for half in halves for term in half] + [row_gap, col_gap]
    if aliased:
        in_specs += [pl.BlockSpec(memory_space=pl.ANY)]
        operands += [out]
    return pl.pallas_call(
        lambda *refs: product_kernel(groups, parts, steps, aliased, *refs),
        grid_spec=pltpu.PrefetchScalarGridSpec(
            num_scalar_prefetch=1,
            grid=(sum(steps),),
            in_specs=in_specs,
            out_specs=pl.BlockSpec((tile, total), lambda m, s: (m + first, chunk)),
            scratch_shapes=[pltpu.VMEM((3 * whole, total), jnp.bfloat16)],
        ),
        out_shape=jax.ShapeDtypeStruct(shape, jnp.float32),
        input_output_aliases={len(operands) - 1: 0} if aliased else {},
        cost_estimate=pl.CostEstimate(
            flops=6 * rows * total * whole, bytes_accessed=4 * rows * (total + whole), transcendentals=0
        ),
        name="product",
    )(*operands)


def swap(x, axis, size, step):
    return lax.ppermute(x, axis, [(j, step(j)) for j in range(size)])


def double(piece, axis, size, steps):
    held = [piece]
    for step in steps:
        for x in list(held):
            held.append(swap(x, axis, size, step))
    return held


def direct(piece, axis, size, offsets):
    return [piece] + [swap(piece, axis, size, lambda j, m=m: j ^ m) for m in offsets[1:]]


def body(amplitudes, integrals, occ_energy, vir_energy):
    virtuals, own = amplitudes.shape[:2]
    rows_size, parts = lax.axis_size("row"), lax.axis_size("col")
    occupied = own * rows_size
    whole = amplitudes.shape[2] * amplitudes.shape[3]
    columns = integrals.shape[1]
    height = virtuals * occupied
    col = lax.axis_index("col")

    starts = [columns * cut // CUTS[-1] for cut in CUTS]
    own_pieces = [integrals[:, a:b] for a, b in zip(starts, starts[1:])]
    order = masks(parts)[::-1]
    steps = [lambda j, bit=bit: j ^ bit for bit in order]
    offsets = [0]
    for bit in order:
        offsets += [m ^ bit for m in offsets]
    where = jnp.stack([col ^ m for m in offsets]).astype(jnp.int32)

    turned = jnp.transpose(amplitudes, (1, 2, 3, 0)).reshape(own, whole, virtuals)
    high, low, wide, row_gap, col_gap = gather(turned, integrals, occ_energy, vir_energy, starts[1])
    half = (high, low)
    chunk1 = double(own_pieces[1], "col", parts, steps)
    chunk2 = direct(own_pieces[2], "col", parts, offsets)
    chunk3 = direct(own_pieces[3], "col", parts, offsets)

    def block(out, where, chunks, start):
        return product(where, chunks, [half], row_gap, col_gap, out, (height, columns), 0, start)

    plain = jnp.zeros((1,), jnp.int32)
    out = block(None, plain, [[wide]], starts[0])
    out = block(out, where, [chunk1], starts[1])
    out = block(out, where, [chunk2], starts[2])
    return block(out, where, [chunk3], starts[3])


def solution(mesh):
    in_specs = (P("col", "row", None, None), P("col", "row"), P(), P())
    out_specs = P("col", "row")
    return jax.shard_map(body, mesh=mesh, in_specs=in_specs, out_specs=out_specs, check_vma=False)
```

```python
import jax
import jax.numpy as jnp
from jax import lax
from jax.experimental import pallas as pl
from jax.experimental.pallas import tpu as pltpu
from jax.sharding import PartitionSpec as P


CUTS = (0, 4, 6, 8)
A_CUTS = 4
W_CUTS = 4
LANES = 128
PAD = 8
GROUP = 8


def masks(size):
    return [1 << j for j in range(size.bit_length() - 1)]


def split(x):
    high = x.astype(jnp.bfloat16)
    return high, (x - high.astype(jnp.float32)).astype(jnp.bfloat16)


def across(index, bit):
    return index + bit - 2 * bit * (index // bit % 2)


def doubling(me, bits):
    held, flows, partners = [me], [], [across(me, bit) for bit in bits]
    for s, bit in enumerate(bits):
        for j, x in enumerate(list(held)):
            flows.append((s, j))
            held.append(across(x, bit))
    return partners, flows, held


def gather_kernel(
    rows_size, parts, amp_ref, w_ref, vir_ref, occ_ref, high_ref, low_ref, wide_ref, row_ref, col_ref,
    land, mixed, high, low, own_w, row_gap, col_gap, send, recv, swap_send, swap_recv, w_send, w_recv, local
):
    row, col = lax.axis_index("row"), lax.axis_index("col")
    own, depth, virtuals = amp_ref.shape
    occupied = own * rows_size
    cut = high.shape[1]
    cuts = depth // cut
    w_rows = w_ref.shape[0]
    w_width = wide_ref.shape[1] // W_CUTS

    def chip_bits(device):
        chip = masks(rows_size)[1:]
        odd = device % 2
        return [a + odd * (b - a) for a, b in zip(chip, chip[::-1])]

    sibling = across(row, 1)
    partners, flows, held = doubling(row, chip_bits(row))
    sibling_held = doubling(sibling, chip_bits(sibling))[2]
    w_partners, w_flows, w_held = doubling(col, masks(parts)[::-1])

    barrier = pltpu.get_barrier_semaphore()
    for device in partners + [sibling]:
        pl.semaphore_signal(barrier, inc=1, device_id=(device, col), device_id_type=pl.DeviceIdType.MESH)
    for device in w_partners:
        pl.semaphore_signal(barrier, inc=1, device_id=(row, device), device_id_type=pl.DeviceIdType.MESH)
    pl.semaphore_wait(barrier, len(partners) + 1 + len(w_partners))

    def part(ref, j):
        return ref.at[:, pl.ds(pl.multiple_of(j * cut, cut), cut), :]

    def remote(source, target, send_sem, recv_sem, device):
        return pltpu.make_async_remote_copy(
            src_ref=source, dst_ref=target, send_sem=send_sem, recv_sem=recv_sem,
            device_id=device, device_id_type=pl.DeviceIdType.MESH,
        )

    def flow(j, e):
        s, q = flows[e]
        source = amp_ref if q == 0 else land.at[held[q]]
        return remote(part(source, j), part(land.at[held[q]], j), send.at[j, e], recv.at[j, e], (partners[s], col))

    def arrival(j, e):
        block = part(land.at[held[e + 1]], j)
        return remote(block, block, send.at[j, e], recv.at[j, e], (sibling, col))

    def across_chip(j, q):
        source = amp_ref if q == 0 else land.at[held[q]]
        return remote(part(source, j), part(land.at[held[q]], j), swap_send.at[j, q], swap_recv.at[j, q], (sibling, col))

    def chip_arrival(j, q):
        block = part(land.at[sibling_held[q]], j)
        return remote(block, block, swap_send.at[j, q], swap_recv.at[j, q], (sibling, col))

    def w_span(k):
        return pl.ds(pl.multiple_of(k * w_width, w_width), w_width)

    def w_block(k, q):
        return wide_ref.at[pl.ds(pl.multiple_of(w_held[q] * w_rows, w_rows), w_rows), w_span(k)]

    def w_flow(k, e):
        s, q = w_flows[e]
        source = w_ref.at[:, w_span(k)] if q == 0 else w_block(k, q)
        return remote(source, w_block(k, q), w_send.at[k, e], w_recv.at[k, e], (row, w_partners[s]))

    def w_arrival(k, e):
        block = w_block(k, e + 1)
        return remote(block, block, w_send.at[k, e], w_recv.at[k, e], (row, w_partners[0]))

    def issue(j):
        for e, (s, q) in enumerate(flows):
            if q == 0:
                flow(j, e).start()
        across_chip(j, 0).start()

    issue(0)
    for s in range(len(w_partners)):
        for k in range(W_CUTS):
            for e, (t, q) in enumerate(w_flows):
                if q == 0 and t == s:
                    w_flow(k, e).start()
        if s == 0 and cuts > 1:
            issue(1)
    mine = pltpu.make_async_copy(amp_ref, land.at[row], local.at[0])
    mine.start()
    w_in = pltpu.make_async_copy(w_ref.at[:, pl.ds(0, W_CUTS * w_width)], own_w, local.at[1])
    w_in.start()
    mine.wait()
    w_in.wait()
    w_out = pltpu.make_async_copy(
        own_w, wide_ref.at[pl.ds(pl.multiple_of(col * w_rows, w_rows), w_rows), :], local.at[1]
    )
    w_out.start()

    blocks, stride = cut // LANES, occupied + PAD
    w_relayed = sorted({q - 1 for _, q in w_flows if q})

    def place(device, j):
        for i in range(own):
            for block in range(blocks):
                x = land[device, i, pl.ds(pl.multiple_of(j * cut + block * LANES, LANES), LANES), :]
                mixed[block, pl.ds(device * own + i, virtuals, stride=stride), :] = jnp.swapaxes(x, 0, 1)

    def store(j):
        span = pl.ds(pl.multiple_of(j * cut, cut), cut)
        return [
            pltpu.make_async_copy(high, high_ref.at[:, span], local.at[2]),
            pltpu.make_async_copy(low, low_ref.at[:, span], local.at[3]),
        ]

    gap_copies = [
        pltpu.make_async_copy(row_gap, row_ref, local.at[4]),
        pltpu.make_async_copy(col_gap, col_ref, local.at[5]),
    ]

    def spread(shape, axis):
        at = lax.broadcasted_iota(jnp.int32, shape, axis) % occupied
        value = jnp.full(shape, occ_ref[0], jnp.float32)
        for i in range(1, occupied):
            value = jnp.where(at >= i, occ_ref[i], value)
        return value

    def gaps():
        down = spread((occupied, LANES), 0)
        along = spread((8, LANES), 1)

        @pl.loop(0, virtuals)
        def _(a):
            rows = pl.ds(pl.multiple_of(a * occupied, occupied), occupied)
            row_gap[rows, :] = vir_ref[col * virtuals + a] - down

        columns = col_gap.shape[1]
        per = LANES // occupied
        place_of = lax.broadcasted_iota(jnp.int32, (8, LANES), 1)

        @pl.loop(0, columns // LANES)
        def _(n):
            first = row * (columns // occupied) + n * per
            value = jnp.full((8, LANES), vir_ref[first], jnp.float32)
            for v in range(1, per):
                value = jnp.where(place_of >= v * occupied, vir_ref[first + v], value)
            col_gap[:, pl.ds(pl.multiple_of(n * LANES, LANES), LANES)] = value - along

        for copy in gap_copies:
            copy.start()

    relayed = sorted({q - 1 for _, q in flows if q})

    def forward(j):
        for e in relayed:
            arrival(j, e).wait_recv()
            for f, (t, p) in enumerate(flows):
                if p == e + 1:
                    flow(j, f).start()
            across_chip(j, e + 1).start()

        @pl.when(j + 2 < cuts)
        def _():
            issue(j + 2)

    forward(0)
    gaps()

    @pl.loop(0, cuts)
    def _(j):
        @pl.when(j + 1 < cuts)
        def _():
            forward(j + 1)

        place(row, j)
        for e in relayed:
            place(held[e + 1], j)
        for n in range(2):
            k = 2 * j + n

            @pl.when(k < W_CUTS)
            def _(k=k):
                for e in w_relayed:
                    w_arrival(k, e).wait_recv()
                    for f, (t, p) in enumerate(w_flows):
                        if p == e + 1:
                            w_flow(k, f).start()
        for e in range(len(flows)):
            if e not in relayed:
                arrival(j, e).wait_recv()
                across_chip(j, e + 1).start()
                place(held[e + 1], j)
        for q in range(len(held)):
            chip_arrival(j, q).wait_recv()
            place(sibling_held[q], j)

        @pl.when(j > 0)
        def _():
            for copy in store(j):
                copy.wait()

        for block in range(blocks):
            lanes = pl.ds(block * LANES, LANES)

            @pl.loop(0, virtuals // GROUP)
            def _(g):
                for n in range(GROUP):
                    a = g * GROUP + n
                    rows = pl.ds(pl.multiple_of(a * occupied, occupied), occupied)
                    x = mixed[block, pl.ds(pl.multiple_of(a * stride, 8), occupied), :]
                    high[rows, lanes], low[rows, lanes] = split(x)

        for copy in store(j):
            copy.start()

    for copy in store(cuts - 1):
        copy.wait()
    w_out.wait()
    for copy in gap_copies:
        copy.wait()
    for k in range(W_CUTS):
        for e in range(len(w_flows)):
            if e not in w_relayed:
                w_arrival(k, e).wait_recv()
    for j in range(cuts):
        for e in range(len(flows)):
            flow(j, e).wait_send()
        for q in range(len(held)):
            across_chip(j, q).wait_send()
    for k in range(W_CUTS):
        for e in range(len(w_flows)):
            w_flow(k, e).wait_send()


def gather(amplitudes, integrals, occ_energy, vir_energy, width):
    own, depth, virtuals = amplitudes.shape
    rows_size, parts = lax.axis_size("row"), lax.axis_size("col")
    occupied = own * rows_size
    cut = depth // A_CUTS
    flows, held, w_flows = rows_size // 2 - 1, rows_size // 2, parts - 1
    terms = jax.ShapeDtypeStruct((occupied * virtuals, depth), jnp.bfloat16)
    wide = jax.ShapeDtypeStruct((parts * integrals.shape[0], width), jnp.float32)
    down = jax.ShapeDtypeStruct((occupied * virtuals, LANES), jnp.float32)
    along = jax.ShapeDtypeStruct((8, integrals.shape[1]), jnp.float32)
    sent = 4 * (amplitudes.size * flows + parts * integrals.shape[0] * width)
    dma = pltpu.SemaphoreType.DMA
    return pl.pallas_call(
        lambda *refs: gather_kernel(rows_size, parts, *refs),
        in_specs=[pl.BlockSpec(memory_space=pl.ANY)] * 2
        + [pl.BlockSpec(memory_space=pltpu.SMEM)] * 2,
        out_specs=[pl.BlockSpec(memory_space=pl.ANY)] * 5,
        out_shape=[terms, terms, wide, down, along],
        scratch_shapes=[
            pltpu.VMEM((rows_size, own, depth, virtuals), jnp.float32),
            pltpu.VMEM((cut // LANES, virtuals * (occupied + PAD), LANES), jnp.float32),
            pltpu.VMEM((occupied * virtuals, cut), jnp.bfloat16),
            pltpu.VMEM((occupied * virtuals, cut), jnp.bfloat16),
            pltpu.VMEM((integrals.shape[0], width), jnp.float32),
            pltpu.VMEM(down.shape, jnp.float32),
            pltpu.VMEM(along.shape, jnp.float32),
            dma((A_CUTS, flows)), dma((A_CUTS, flows)),
            dma((A_CUTS, held)), dma((A_CUTS, held)),
            dma((W_CUTS, w_flows)), dma((W_CUTS, w_flows)),
            dma((6,)),
        ],
        compiler_params=pltpu.CompilerParams(
            collective_id=0, has_side_effects=True, vmem_limit_bytes=60 * 1024 * 1024
        ),
        cost_estimate=pl.CostEstimate(flops=0, bytes_accessed=sent * 8, transcendentals=0),
        name="gather",
    )(
        amplitudes,
        integrals,
        vir_energy,
        occ_energy,
    )


def product_kernel(groups, parts, steps, aliased, where_ref, *refs):
    count, halves = groups * parts, len(steps)
    pieces, refs = refs[:count], refs[count:]
    terms, refs = refs[: 2 * halves], refs[2 * halves :]
    row_ref, col_ref = refs[:2]
    out_ref, w_ref = refs[2 + aliased :]
    depth, width = pieces[0].shape
    whole = parts * depth
    m = pl.program_id(0)

    @pl.when(m == 0)
    def _():
        for j, piece in enumerate(pieces):
            start = pl.multiple_of(where_ref[j % parts] * depth, depth)
            lanes = pl.ds(j // parts * width, width)
            w_high, w_low = split(piece[...])
            w_ref[pl.ds(start, depth), lanes] = w_high
            w_ref[pl.ds(start + whole, depth), lanes] = w_high
            w_ref[pl.ds(start + 2 * whole, depth), lanes] = w_low

    def multiply(high_ref, low_ref):
        high = high_ref[...]
        both = jnp.concatenate([high, low_ref[...], high], axis=1)
        total = jnp.dot(both, w_ref[...], preferred_element_type=jnp.float32)
        out_ref[...] = total / (row_ref[:, :1] + col_ref[:1, :])

    if halves == 1:
        multiply(*terms)
    else:
        stop = 0
        for h, step in enumerate(steps):
            start, stop = stop, stop + step
            pl.when((m >= start) & (m < stop))(lambda h=h: multiply(terms[2 * h], terms[2 * h + 1]))


def product(where, chunks, halves, row_gap, col_gap, out, shape, top, start):
    groups, parts = len(chunks), len(chunks[0])
    depth, width = chunks[0][0].shape
    total = groups * width
    whole = halves[0][0].shape[1]
    tile = min(512 if total > 256 else 1024, halves[0][0].shape[0])
    steps = [high.shape[0] // tile for high, _ in halves]
    rows = sum(steps) * tile
    first, chunk = top // tile, start // total
    aliased = 0 if out is None else 1
    in_specs = [pl.BlockSpec((depth, width), lambda m, s: (0, 0), pipeline_mode=pl.Buffered(1))] * (groups * parts)
    before = 0
    for step in steps:
        index = lambda m, s, before=before, step=step: (jnp.clip(m - before, 0, step - 1), 0)
        in_specs += [pl.BlockSpec((tile, whole), index)] * 2
        before += step
    in_specs += [pl.BlockSpec((tile, LANES), lambda m, s: (m + first, 0))]
    in_specs += [pl.BlockSpec((8, total), lambda m, s: (0, chunk))]
    operands = [where, *(piece for pieces in chunks for piece in pieces)]
    operands += [term for half in halves for term in half] + [row_gap, col_gap]
    if aliased:
        in_specs += [pl.BlockSpec(memory_space=pl.ANY)]
        operands += [out]
    return pl.pallas_call(
        lambda *refs: product_kernel(groups, parts, steps, aliased, *refs),
        grid_spec=pltpu.PrefetchScalarGridSpec(
            num_scalar_prefetch=1,
            grid=(sum(steps),),
            in_specs=in_specs,
            out_specs=pl.BlockSpec((tile, total), lambda m, s: (m + first, chunk)),
            scratch_shapes=[pltpu.VMEM((3 * whole, total), jnp.bfloat16)],
        ),
        out_shape=jax.ShapeDtypeStruct(shape, jnp.float32),
        input_output_aliases={len(operands) - 1: 0} if aliased else {},
        cost_estimate=pl.CostEstimate(
            flops=6 * rows * total * whole, bytes_accessed=4 * rows * (total + whole), transcendentals=0
        ),
        name="product",
    )(*operands)


def swap(x, axis, size, step):
    return lax.ppermute(x, axis, [(j, step(j)) for j in range(size)])


def double(piece, axis, size, steps):
    held = [piece]
    for step in steps:
        for x in list(held):
            held.append(swap(x, axis, size, step))
    return held


def body(amplitudes, integrals, occ_energy, vir_energy):
    virtuals, own = amplitudes.shape[:2]
    rows_size, parts = lax.axis_size("row"), lax.axis_size("col")
    occupied = own * rows_size
    whole = amplitudes.shape[2] * amplitudes.shape[3]
    columns = integrals.shape[1]
    height = virtuals * occupied
    col = lax.axis_index("col")

    starts = [columns * cut // CUTS[-1] for cut in CUTS]
    own_pieces = [integrals[:, a:b] for a, b in zip(starts, starts[1:])]
    order = masks(parts)[::-1]
    steps = [lambda j, bit=bit: j ^ bit for bit in order]
    offsets = [0]
    for bit in order:
        offsets += [m ^ bit for m in offsets]
    where = jnp.stack([col ^ m for m in offsets]).astype(jnp.int32)

    turned = jnp.transpose(amplitudes, (1, 2, 3, 0)).reshape(own, whole, virtuals)
    high, low, wide, row_gap, col_gap = gather(turned, integrals, occ_energy, vir_energy, starts[1])
    half = (high, low)
    chunk1 = double(own_pieces[1], "col", parts, steps)
    chunk2 = double(own_pieces[2], "col", parts, steps)

    def block(out, where, chunks, start):
        return product(where, chunks, [half], row_gap, col_gap, out, (height, columns), 0, start)

    plain = jnp.zeros((1,), jnp.int32)
    out = block(None, plain, [[wide]], starts[0])
    out = block(out, where, [chunk1], starts[1])
    return block(out, where, [chunk2], starts[2])


def solution(mesh):
    in_specs = (P("col", "row", None, None), P("col", "row"), P(), P())
    out_specs = P("col", "row")
    return jax.shard_map(body, mesh=mesh, in_specs=in_specs, out_specs=out_specs, check_vma=False)
```

```python
import jax
import jax.numpy as jnp
from jax import lax
from jax.experimental import pallas as pl
from jax.experimental.pallas import tpu as pltpu
from jax.sharding import PartitionSpec as P


CUTS = (0, 4, 6, 8)
A_CUTS = 4
W_CUTS = 4
LANES = 128
PAD = 8
GROUP = 8


def masks(size):
    return [1 << j for j in range(size.bit_length() - 1)]


def split(x):
    high = x.astype(jnp.bfloat16)
    return high, (x - high.astype(jnp.float32)).astype(jnp.bfloat16)


def across(index, bit):
    return index + bit - 2 * bit * (index // bit % 2)


def doubling(me, bits):
    held, flows, partners = [me], [], [across(me, bit) for bit in bits]
    for s, bit in enumerate(bits):
        for j, x in enumerate(list(held)):
            flows.append((s, j))
            held.append(across(x, bit))
    return partners, flows, held


def gather_kernel(
    rows_size, parts, amp_ref, w_ref, vir_ref, occ_ref, high_ref, low_ref, wide_ref, row_ref, col_ref,
    land, mixed, high, low, own_w, row_gap, col_gap, send, recv, swap_send, swap_recv, w_send, w_recv, local
):
    row, col = lax.axis_index("row"), lax.axis_index("col")
    own, depth, virtuals = amp_ref.shape
    occupied = own * rows_size
    cut = high.shape[1]
    cuts = depth // cut
    w_rows = w_ref.shape[0]
    w_width = wide_ref.shape[1] // W_CUTS

    def chip_bits(device):
        chip = masks(rows_size)[1:]
        odd = device % 2
        return [a + odd * (b - a) for a, b in zip(chip, chip[::-1])]

    sibling = across(row, 1)
    partners, flows, held = doubling(row, chip_bits(row))
    sibling_held = doubling(sibling, chip_bits(sibling))[2]
    w_partners, w_flows, w_held = doubling(col, masks(parts)[::-1])

    barrier = pltpu.get_barrier_semaphore()
    for device in partners + [sibling]:
        pl.semaphore_signal(barrier, inc=1, device_id=(device, col), device_id_type=pl.DeviceIdType.MESH)
    for device in w_partners:
        pl.semaphore_signal(barrier, inc=1, device_id=(row, device), device_id_type=pl.DeviceIdType.MESH)
    pl.semaphore_wait(barrier, len(partners) + 1 + len(w_partners))

    def part(ref, j):
        return ref.at[:, pl.ds(pl.multiple_of(j * cut, cut), cut), :]

    def remote(source, target, send_sem, recv_sem, device):
        return pltpu.make_async_remote_copy(
            src_ref=source, dst_ref=target, send_sem=send_sem, recv_sem=recv_sem,
            device_id=device, device_id_type=pl.DeviceIdType.MESH,
        )

    def flow(j, e):
        s, q = flows[e]
        source = amp_ref if q == 0 else land.at[held[q]]
        return remote(part(source, j), part(land.at[held[q]], j), send.at[j, e], recv.at[j, e], (partners[s], col))

    def arrival(j, e):
        block = part(land.at[held[e + 1]], j)
        return remote(block, block, send.at[j, e], recv.at[j, e], (sibling, col))

    def across_chip(j, q):
        source = amp_ref if q == 0 else land.at[held[q]]
        return remote(part(source, j), part(land.at[held[q]], j), swap_send.at[j, q], swap_recv.at[j, q], (sibling, col))

    def chip_arrival(j, q):
        block = part(land.at[sibling_held[q]], j)
        return remote(block, block, swap_send.at[j, q], swap_recv.at[j, q], (sibling, col))

    def w_span(k):
        return pl.ds(pl.multiple_of(k * w_width, w_width), w_width)

    def w_block(k, q):
        return wide_ref.at[pl.ds(pl.multiple_of(w_held[q] * w_rows, w_rows), w_rows), w_span(k)]

    def w_flow(k, e):
        s, q = w_flows[e]
        source = w_ref.at[:, w_span(k)] if q == 0 else w_block(k, q)
        return remote(source, w_block(k, q), w_send.at[k, e], w_recv.at[k, e], (row, w_partners[s]))

    def w_arrival(k, e):
        block = w_block(k, e + 1)
        return remote(block, block, w_send.at[k, e], w_recv.at[k, e], (row, w_partners[0]))

    def issue(j):
        for e, (s, q) in enumerate(flows):
            if q == 0:
                flow(j, e).start()
        across_chip(j, 0).start()

    issue(0)
    for s in range(len(w_partners)):
        for k in range(W_CUTS):
            for e, (t, q) in enumerate(w_flows):
                if q == 0 and t == s:
                    w_flow(k, e).start()
        if s == 0 and cuts > 1:
            issue(1)
    mine = pltpu.make_async_copy(amp_ref, land.at[row], local.at[0])
    mine.start()
    w_in = pltpu.make_async_copy(w_ref.at[:, pl.ds(0, W_CUTS * w_width)], own_w, local.at[1])
    w_in.start()
    mine.wait()
    w_in.wait()
    w_out = pltpu.make_async_copy(
        own_w, wide_ref.at[pl.ds(pl.multiple_of(col * w_rows, w_rows), w_rows), :], local.at[1]
    )
    w_out.start()

    blocks, stride = cut // LANES, occupied + PAD
    w_relayed = sorted({q - 1 for _, q in w_flows if q})

    def place(device, j):
        for i in range(own):
            for block in range(blocks):
                x = land[device, i, pl.ds(pl.multiple_of(j * cut + block * LANES, LANES), LANES), :]
                mixed[block, pl.ds(device * own + i, virtuals, stride=stride), :] = jnp.swapaxes(x, 0, 1)

    def store(j):
        span = pl.ds(pl.multiple_of(j * cut, cut), cut)
        return [
            pltpu.make_async_copy(high, high_ref.at[:, span], local.at[2]),
            pltpu.make_async_copy(low, low_ref.at[:, span], local.at[3]),
        ]

    gap_copies = [
        pltpu.make_async_copy(row_gap, row_ref, local.at[4]),
        pltpu.make_async_copy(col_gap, col_ref, local.at[5]),
    ]

    def spread(shape, axis):
        at = lax.broadcasted_iota(jnp.int32, shape, axis) % occupied
        value = jnp.full(shape, occ_ref[0], jnp.float32)
        for i in range(1, occupied):
            value = jnp.where(at >= i, occ_ref[i], value)
        return value

    def gaps():
        down = spread((occupied, LANES), 0)
        along = spread((8, LANES), 1)

        @pl.loop(0, virtuals)
        def _(a):
            rows = pl.ds(pl.multiple_of(a * occupied, occupied), occupied)
            row_gap[rows, :] = vir_ref[col * virtuals + a] - down

        columns = col_gap.shape[1]
        per = LANES // occupied
        place_of = lax.broadcasted_iota(jnp.int32, (8, LANES), 1)

        @pl.loop(0, columns // LANES)
        def _(n):
            first = row * (columns // occupied) + n * per
            value = jnp.full((8, LANES), vir_ref[first], jnp.float32)
            for v in range(1, per):
                value = jnp.where(place_of >= v * occupied, vir_ref[first + v], value)
            col_gap[:, pl.ds(pl.multiple_of(n * LANES, LANES), LANES)] = value - along

        for copy in gap_copies:
            copy.start()

    relayed = sorted({q - 1 for _, q in flows if q})

    def forward(j):
        for e in relayed:
            arrival(j, e).wait_recv()
            for f, (t, p) in enumerate(flows):
                if p == e + 1:
                    flow(j, f).start()
            across_chip(j, e + 1).start()

        @pl.when(j + 2 < cuts)
        def _():
            issue(j + 2)

    forward(0)
    gaps()

    @pl.loop(0, cuts)
    def _(j):
        @pl.when(j + 1 < cuts)
        def _():
            forward(j + 1)

        place(row, j)
        for e in relayed:
            place(held[e + 1], j)
        for n in range(2):
            k = 2 * j + n

            @pl.when(k < W_CUTS)
            def _(k=k):
                for e in w_relayed:
                    w_arrival(k, e).wait_recv()
                    for f, (t, p) in enumerate(w_flows):
                        if p == e + 1:
                            w_flow(k, f).start()
        for e in range(len(flows)):
            if e not in relayed:
                arrival(j, e).wait_recv()
                across_chip(j, e + 1).start()
                place(held[e + 1], j)
        for q in range(len(held)):
            chip_arrival(j, q).wait_recv()
            place(sibling_held[q], j)

        @pl.when(j > 0)
        def _():
            for copy in store(j):
                copy.wait()

        for block in range(blocks):
            lanes = pl.ds(block * LANES, LANES)

            @pl.loop(0, virtuals // GROUP)
            def _(g):
                for n in range(GROUP):
                    a = g * GROUP + n
                    rows = pl.ds(pl.multiple_of(a * occupied, occupied), occupied)
                    x = mixed[block, pl.ds(pl.multiple_of(a * stride, 8), occupied), :]
                    high[rows, lanes], low[rows, lanes] = split(x)

        for copy in store(j):
            copy.start()

    for copy in store(cuts - 1):
        copy.wait()
    w_out.wait()
    for copy in gap_copies:
        copy.wait()
    for k in range(W_CUTS):
        for e in range(len(w_flows)):
            if e not in w_relayed:
                w_arrival(k, e).wait_recv()
    for j in range(cuts):
        for e in range(len(flows)):
            flow(j, e).wait_send()
        for q in range(len(held)):
            across_chip(j, q).wait_send()
    for k in range(W_CUTS):
        for e in range(len(w_flows)):
            w_flow(k, e).wait_send()


def gather(amplitudes, integrals, occ_energy, vir_energy, width):
    own, depth, virtuals = amplitudes.shape
    rows_size, parts = lax.axis_size("row"), lax.axis_size("col")
    occupied = own * rows_size
    cut = depth // A_CUTS
    flows, held, w_flows = rows_size // 2 - 1, rows_size // 2, parts - 1
    terms = jax.ShapeDtypeStruct((occupied * virtuals, depth), jnp.bfloat16)
    wide = jax.ShapeDtypeStruct((parts * integrals.shape[0], width), jnp.float32)
    down = jax.ShapeDtypeStruct((occupied * virtuals, LANES), jnp.float32)
    along = jax.ShapeDtypeStruct((8, integrals.shape[1]), jnp.float32)
    sent = 4 * (amplitudes.size * flows + parts * integrals.shape[0] * width)
    dma = pltpu.SemaphoreType.DMA
    return pl.pallas_call(
        lambda *refs: gather_kernel(rows_size, parts, *refs),
        in_specs=[pl.BlockSpec(memory_space=pl.ANY)] * 2
        + [pl.BlockSpec(memory_space=pltpu.SMEM)] * 2,
        out_specs=[pl.BlockSpec(memory_space=pl.ANY)] * 5,
        out_shape=[terms, terms, wide, down, along],
        scratch_shapes=[
            pltpu.VMEM((rows_size, own, depth, virtuals), jnp.float32),
            pltpu.VMEM((cut // LANES, virtuals * (occupied + PAD), LANES), jnp.float32),
            pltpu.VMEM((occupied * virtuals, cut), jnp.bfloat16),
            pltpu.VMEM((occupied * virtuals, cut), jnp.bfloat16),
            pltpu.VMEM((integrals.shape[0], width), jnp.float32),
            pltpu.VMEM(down.shape, jnp.float32),
            pltpu.VMEM(along.shape, jnp.float32),
            dma((A_CUTS, flows)), dma((A_CUTS, flows)),
            dma((A_CUTS, held)), dma((A_CUTS, held)),
            dma((W_CUTS, w_flows)), dma((W_CUTS, w_flows)),
            dma((6,)),
        ],
        compiler_params=pltpu.CompilerParams(
            collective_id=0, has_side_effects=True, vmem_limit_bytes=60 * 1024 * 1024
        ),
        cost_estimate=pl.CostEstimate(flops=0, bytes_accessed=sent * 8, transcendentals=0),
        name="gather",
    )(
        amplitudes,
        integrals,
        vir_energy,
        occ_energy,
    )


def product_kernel(groups, parts, steps, aliased, where_ref, *refs):
    count, halves = groups * parts, len(steps)
    pieces, refs = refs[:count], refs[count:]
    terms, refs = refs[: 2 * halves], refs[2 * halves :]
    row_ref, col_ref = refs[:2]
    out_ref, w_ref = refs[2 + aliased :]
    depth, width = pieces[0].shape
    whole = parts * depth
    m = pl.program_id(0)

    @pl.when(m == 0)
    def _():
        origin = doubling(lax.axis_index("col"), masks(parts)[::-1])[2] if parts > 1 else [0]
        for j, piece in enumerate(pieces):
            start = pl.multiple_of(origin[j % parts] * depth, depth)
            lanes = pl.ds(j // parts * width, width)
            w_high, w_low = split(piece[...])
            w_ref[pl.ds(start, depth), lanes] = w_high
            w_ref[pl.ds(start + whole, depth), lanes] = w_high
            w_ref[pl.ds(start + 2 * whole, depth), lanes] = w_low

    def multiply(high_ref, low_ref):
        high = high_ref[...]
        both = jnp.concatenate([high, low_ref[...], high], axis=1)
        total = jnp.dot(both, w_ref[...], preferred_element_type=jnp.float32)
        out_ref[...] = total / (row_ref[:, :1] + col_ref[:1, :])

    if halves == 1:
        multiply(*terms)
    else:
        stop = 0
        for h, step in enumerate(steps):
            start, stop = stop, stop + step
            pl.when((m >= start) & (m < stop))(lambda h=h: multiply(terms[2 * h], terms[2 * h + 1]))


def product(where, chunks, halves, row_gap, col_gap, out, shape, top, start):
    groups, parts = len(chunks), len(chunks[0])
    depth, width = chunks[0][0].shape
    total = groups * width
    whole = halves[0][0].shape[1]
    tile = min(512 if total > 256 else 1024, halves[0][0].shape[0])
    steps = [high.shape[0] // tile for high, _ in halves]
    rows = sum(steps) * tile
    first, chunk = top // tile, start // total
    aliased = 0 if out is None else 1
    in_specs = [pl.BlockSpec((depth, width), lambda m, s: (0, 0), pipeline_mode=pl.Buffered(1))] * (groups * parts)
    before = 0
    for step in steps:
        index = lambda m, s, before=before, step=step: (jnp.clip(m - before, 0, step - 1), 0)
        in_specs += [pl.BlockSpec((tile, whole), index)] * 2
        before += step
    in_specs += [pl.BlockSpec((tile, LANES), lambda m, s: (m + first, 0))]
    in_specs += [pl.BlockSpec((8, total), lambda m, s: (0, chunk))]
    operands = [where, *(piece for pieces in chunks for piece in pieces)]
    operands += [term for half in halves for term in half] + [row_gap, col_gap]
    if aliased:
        in_specs += [pl.BlockSpec(memory_space=pl.ANY)]
        operands += [out]
    return pl.pallas_call(
        lambda *refs: product_kernel(groups, parts, steps, aliased, *refs),
        grid_spec=pltpu.PrefetchScalarGridSpec(
            num_scalar_prefetch=1,
            grid=(sum(steps),),
            in_specs=in_specs,
            out_specs=pl.BlockSpec((tile, total), lambda m, s: (m + first, chunk)),
            scratch_shapes=[pltpu.VMEM((3 * whole, total), jnp.bfloat16)],
        ),
        out_shape=jax.ShapeDtypeStruct(shape, jnp.float32),
        input_output_aliases={len(operands) - 1: 0} if aliased else {},
        cost_estimate=pl.CostEstimate(
            flops=6 * rows * total * whole, bytes_accessed=4 * rows * (total + whole), transcendentals=0
        ),
        name="product",
    )(*operands)


def swap(x, axis, size, step):
    return lax.ppermute(x, axis, [(j, step(j)) for j in range(size)])


def double(piece, axis, size, steps):
    held = [piece]
    for step in steps:
        for x in list(held):
            held.append(swap(x, axis, size, step))
    return held


def body(amplitudes, integrals, occ_energy, vir_energy):
    virtuals, own = amplitudes.shape[:2]
    rows_size, parts = lax.axis_size("row"), lax.axis_size("col")
    occupied = own * rows_size
    whole = amplitudes.shape[2] * amplitudes.shape[3]
    columns = integrals.shape[1]
    height = virtuals * occupied
    col = lax.axis_index("col")

    starts = [columns * cut // CUTS[-1] for cut in CUTS]
    own_pieces = [integrals[:, a:b] for a, b in zip(starts, starts[1:])]
    order = masks(parts)[::-1]
    steps = [lambda j, bit=bit: j ^ bit for bit in order]
    offsets = [0]
    for bit in order:
        offsets += [m ^ bit for m in offsets]
    where = jnp.stack([col ^ m for m in offsets]).astype(jnp.int32)

    turned = jnp.transpose(amplitudes, (1, 2, 3, 0)).reshape(own, whole, virtuals)
    high, low, wide, row_gap, col_gap = gather(turned, integrals, occ_energy, vir_energy, starts[1])
    half = (high, low)
    chunk1 = double(own_pieces[1], "col", parts, steps)
    chunk2 = double(own_pieces[2], "col", parts, steps)

    def block(out, where, chunks, start):
        return product(where, chunks, [half], row_gap, col_gap, out, (height, columns), 0, start)

    plain = jnp.zeros((1,), jnp.int32)
    out = block(None, plain, [[wide]], starts[0])
    out = block(out, plain, [chunk1], starts[1])
    return block(out, plain, [chunk2], starts[2])


def solution(mesh):
    in_specs = (P("col", "row", None, None), P("col", "row"), P(), P())
    out_specs = P("col", "row")
    return jax.shard_map(body, mesh=mesh, in_specs=in_specs, out_specs=out_specs, check_vma=False)
```
